512 devices in a mesh: apa: 16 (over y, core), wire: 32 (over z, x).
Axes of the slice: x: 4, y: 8, z: 8, core: 2. Of those that a mesh axis runs over, the one named last changes fastest.
Arguments:
- ind_frames: bfloat16 [16, 2, 800, 1024], P('apa', None, 'wire'), may hold values from -6 to 6
- col_frames: bfloat16 [16, 960, 1024], P('apa', 'wire'), may hold values from -6 to 6
- ind_kernel: bfloat16 [2, 11, 256], replicated, may hold values from -0.109375 to 0.109375
- col_kernel: bfloat16 [11, 256], replicated, may hold values from -0.109375 to 0.109375
- cell_u: int32 [16, 32, 512], P('apa', 'wire'), may hold values from 0 to 799
- cell_v: int32 [16, 32, 512], P('apa', 'wire'), may hold values from 0 to 799
- cell_w: int32 [16, 32, 512], P('apa', 'wire'), may hold values from 0 to 959
- tile_counts: int32 [16, 32], P('apa', 'wire'), may hold values from 128 to 512, as said below
Outputs:
- cell_charge: float32 [16, 32, 8, 512], P('apa', 'wire')
The draws below stay inside these ranges and needn't reach their ends.
Inputs may be any that keep to these rules, and one draw needn't show every extreme that they name: `tile_counts`: each tile holds 512, 256, 170 or 128 live cells, and in every draw some tile holds exactly 512. `cell_u`: slots past a tile's live count also hold wire numbers of the plane.
All inputs are finite; a program needn't handle non-finite values.
Results may differ from the reference program's by a relative error of at most 0.0003.
Values may be sent and summed in bfloat16 or wider, within the bound.
No kernel may reach another device: no remote copies, remote signals or barrier semaphores. Data moves between devices by JAX's collectives and lax.ppermute only.
A program may use at most 64 MiB of HBM per device.

```python
import jax
import jax.numpy as jnp
from jax import lax

APAS = 16
IND_WIRES = 800
COL_WIRES = 960
REACH = 5
TAPS = 256
BINS_DEV = 8
TILES = 32
TICKS = 1024
CELLS = 512


def draw_tile_counts(key, part):
    first_key, second_key = jax.random.split(jax.random.fold_in(key, 17))
    divisor = jax.random.randint(first_key, (APAS * TILES,), 1, 5)
    counts = CELLS // divisor
    chosen = jax.random.randint(second_key, (), 0, APAS * TILES)
    flattened = jnp.where(jnp.arange(APAS * TILES) == chosen, CELLS, counts)
    return flattened.reshape(APAS, TILES).astype(jnp.int32)


def with_ends(result, stream_key, smallest, largest):
    index_at = [jax.random.randint(jax.random.fold_in(stream_key, axis), (), 0, length) for axis, length in enumerate(result.shape)]
    longest = result.shape.index(max(result.shape))
    neighbour = index_at[:longest] + [(index_at[longest] + 1) % result.shape[longest]] + index_at[longest + 1:]
    return result.at[tuple(index_at)].set(smallest).at[tuple(neighbour)].set(largest)


def block_scale(stream_key, dims, pieces, low, largest):
    level, own = 1.0, jax.random.fold_in(stream_key, 6)
    for position, parts in pieces:
        draws = jnp.exp(jax.random.uniform(jax.random.fold_in(own, position), (parts,), jnp.float32, low / len(pieces), largest / len(pieces)))
        level = level * jnp.repeat(draws, dims[position] // parts).reshape([-1 if axis == position else 1 for axis in range(len(dims))])
    return level


def normal_values(rng, extent, scale, most, cuts=(), kind=jnp.bfloat16):
    entries = scale * jax.random.normal(rng, extent, jnp.float32)
    if cuts:
        entries = entries * block_scale(rng, extent, cuts, -0.22, 0.18)
    return jnp.clip(entries, -most, most).astype(kind)


def setup_inputs(seed: int = 0) -> dict:
    key_of = jax.random.split(jax.random.key(seed), 9)
    ind_frames = normal_values(key_of[0], (APAS, 2, IND_WIRES, TICKS), 1.0, 6.0, ((0, 16), (2, 32)))
    col_frames = normal_values(key_of[1], (APAS, COL_WIRES, TICKS), 1.0, 6.0, ((0, 16), (1, 32)))
    ind_kernel = normal_values(key_of[2], (2, 2 * REACH + 1, TAPS), ((2 * REACH + 1) * TAPS) ** -0.5, 0.109375)
    col_kernel = normal_values(key_of[3], (2 * REACH + 1, TAPS), ((2 * REACH + 1) * TAPS) ** -0.5, 0.109375)
    cell_u = with_ends(jax.random.randint(key_of[4], (APAS, TILES, CELLS), 0, IND_WIRES), jax.random.fold_in(key_of[4], 1), 0, IND_WIRES - 1).astype(jnp.int32)
    cell_v = with_ends(jax.random.randint(key_of[5], (APAS, TILES, CELLS), 0, IND_WIRES), jax.random.fold_in(key_of[5], 1), 0, IND_WIRES - 1).astype(jnp.int32)
    cell_w = with_ends(jax.random.randint(key_of[6], (APAS, TILES, CELLS), 0, COL_WIRES), jax.random.fold_in(key_of[6], 1), 0, COL_WIRES - 1).astype(jnp.int32)
    tile_counts = draw_tile_counts(jax.random.fold_in(key_of[8], 71), 0)
    return dict(ind_frames=ind_frames, col_frames=col_frames, ind_kernel=ind_kernel, col_kernel=col_kernel, cell_u=cell_u, cell_v=cell_v, cell_w=cell_w, tile_counts=tile_counts)


def deconvolve_planes(frames, kernel):
    wire_reach = (kernel.shape[1] - 1) // 2
    tick_count = frames.shape[-1]
    wire_count = frames.shape[2]
    length = tick_count + kernel.shape[-1]
    kernel_spectra = jnp.fft.rfft(kernel.astype(jnp.float32), n=length, axis=-1)

    def one_assembly(single):
        spectra = jnp.fft.rfft(single.astype(jnp.float32), n=length, axis=-1)
        spectra = jnp.pad(spectra, ((0, 0), (wire_reach, wire_reach), (0, 0)))
        summed = spectra[:, 0:wire_count] * kernel_spectra[:, 0, None, :]
        for offset in range(1, 2 * wire_reach + 1):
            summed = summed + spectra[:, offset:offset + wire_count] * kernel_spectra[:, offset, None, :]
        return jnp.fft.irfft(summed, n=length, axis=-1)[..., :tick_count]

    return lax.map(one_assembly, frames)


def reference(ind_frames, col_frames, ind_kernel, col_kernel, cell_u, cell_v, cell_w, tile_counts):
    ind_clean = deconvolve_planes(ind_frames, ind_kernel)
    col_clean = deconvolve_planes(col_frames[:, None], col_kernel[None])[:, 0]
    apa_count = ind_clean.shape[0]
    ind_width = ind_clean.shape[2]
    tick_count = ind_clean.shape[3]
    ind_bins = ind_clean.reshape(apa_count, 2, ind_width, tick_count // 4, 4).sum(axis=-1)
    col_bins = col_clean.reshape(apa_count, col_clean.shape[1], tick_count // 4, 4).sum(axis=-1)

    def per_tile(binned):
        shaped = binned.reshape(apa_count, binned.shape[1], TILES, BINS_DEV)
        return jnp.transpose(shaped, (0, 2, 3, 1))

    def lookup(table, index):
        spread = jnp.broadcast_to(index[:, :, None, :].astype(jnp.int32), (apa_count, TILES, BINS_DEV, CELLS))
        return jnp.take_along_axis(table, spread, axis=3)

    first_plane = lookup(per_tile(ind_bins[:, 0]), cell_u)
    second_plane = lookup(per_tile(ind_bins[:, 1]), cell_v)
    third_plane = lookup(per_tile(col_bins), cell_w)
    charge = jnp.minimum(jnp.minimum(first_plane, second_plane), third_plane)
    live = jnp.arange(CELLS, dtype=jnp.int32)[None, None, None, :] < tile_counts[:, :, None, None]
    return jnp.where(live, charge, jnp.zeros_like(charge))
```

```python
import jax
import jax.numpy as jnp
from jax import lax
from jax.experimental import pallas as pl
from jax.experimental.pallas import tpu as pltpu
from jax.sharding import PartitionSpec as P

LANES = 128
SUB = 8
REBIN = 4
GROUP = 32


def lane_iota(shape=(SUB, LANES)):
    return lax.broadcasted_iota(jnp.int32, shape, 1)


def between(lanes, low, high):
    return (lanes >= low) & (lanes < high)


def segments(widths, reach):
    starts, at = [], 0
    for width in widths:
        starts.append(at + reach)
        at += width + 2 * reach
    return starts


def conv_kernel(reach, indf, colf, indk, colk, out, kmat, toep, wide):
    taps = indk.shape[2]
    offsets = indk.shape[1]
    ticks = indf.shape[3]
    window = taps + LANES
    blocks = ticks // LANES
    bins = LANES // REBIN
    widths = (indf.shape[2], indf.shape[2], colf.shape[1])
    frames = (lambda: indf[0, 0], lambda: indf[0, 1], lambda: colf[0])

    kmat[...] = jnp.zeros_like(kmat)
    kmat[0:offsets, :] = indk[0]
    kmat[16:16 + offsets, :] = indk[1]
    kmat[32:32 + offsets, :] = colk[...]
    total = (lax.broadcasted_iota(jnp.int32, (taps, window), 0)
             + lax.broadcasted_iota(jnp.int32, (taps, window), 1))
    fold = between(total, taps, taps + REBIN).astype(jnp.float32).astype(jnp.bfloat16)
    rows = jnp.dot(kmat[...], fold, preferred_element_type=jnp.float32)

    lanes = lane_iota()
    subs = lax.broadcasted_iota(jnp.int32, (SUB, LANES), 0)
    pieces = window // LANES
    starts = segments(widths, reach)

    sums = []
    for plane in range(3):
        for offset in range(offsets):
            at = 16 * plane + offset
            flat = [jnp.broadcast_to(rows[at:at + 1, LANES * i:LANES * (i + 1)], (SUB, LANES))
                    for i in range(pieces)]
            made = []
            for part in range(bins // SUB):
                base = part * SUB * REBIN
                turned = [pltpu.roll(piece, base, 1, stride=REBIN, stride_axis=0) for piece in flat]
                keep = lanes >= base + REBIN * subs
                before = [jnp.zeros_like(turned[0])] + turned[:-1]
                made.append([jnp.where(keep, a, b) for a, b in zip(turned, before)])
            for pair in range(0, len(made), 2):
                at_row = offset * bins + pair * SUB
                for i in range(pieces):
                    exact = jnp.concatenate([made[pair][i], made[pair + 1][i]], axis=0)
                    high = exact.astype(jnp.bfloat16)
                    low = (exact - high.astype(jnp.float32)).astype(jnp.bfloat16)
                    toep[plane, at_row:at_row + 16, LANES * i:LANES * (i + 1)] = high
                    toep[plane, at_row:at_row + 16, window + LANES * i:window + LANES * (i + 1)] = low

        width = widths[plane]
        mine = frames[plane]()
        zeros = jnp.zeros((GROUP - width, ticks), jnp.bfloat16)
        padded = jnp.concatenate([mine, zeros], axis=0)
        blank = jnp.zeros((GROUP, LANES), jnp.bfloat16)
        history = taps // LANES
        tiles = [blank] * history + [padded[:, LANES * i:LANES * (i + 1)] for i in range(blocks)]
        for block in range(blocks):
            for i in range(pieces):
                piece = tiles[block + i]
                wide[plane, GROUP * block:GROUP * (block + 1), LANES * i:LANES * (i + 1)] = piece
                wide[plane, GROUP * block:GROUP * (block + 1), window + LANES * i:window + LANES * (i + 1)] = piece
        grid = lax.dot_general(
            toep[plane], wide[plane], (((1,), (1,)), ((), ())),
            preferred_element_type=jnp.float32)
        sums.append(grid)

    per_half = LANES // GROUP
    for half in range(blocks // per_half):
        for part in range(bins // SUB):
            gathered = []
            for plane in range(3):
                width = widths[plane]

                def moved(shift):
                    at_row = (reach - shift) * bins + part * SUB
                    piece = sums[plane][at_row:at_row + SUB, LANES * half:LANES * (half + 1)]
                    return piece if shift == 0 else pltpu.roll(piece, shift % LANES, 1)

                spare = GROUP - width
                runs, shift = [], 0
                while shift <= reach:
                    last = min(reach, shift + spare if shift > 0 else spare)
                    runs.append((shift, last))
                    shift = last + 1
                shift = 1
                while shift <= reach:
                    last = min(reach, shift + spare)
                    runs.append((-last, -shift))
                    shift = last + 1
                for first, last in runs:
                    acc = moved(first)
                    for step in range(first + 1, last + 1):
                        acc = acc + moved(step)
                    gathered.append((plane, first, last + width, acc))
            for spot in range(per_half):
                tile = (half * per_half + spot) * (bins // SUB) + part
                result = jnp.zeros((SUB, LANES), jnp.float32)
                for plane, first, end, acc in gathered:
                    start = starts[plane]
                    placed = pltpu.roll(acc, (start - GROUP * spot) % LANES, 1)
                    valid = between(lanes, start + first, start + end)
                    result = result + jnp.where(valid, placed, 0.0)
                out[tile] = result


def cell_kernel(reach, widths, counts, cell_u, cell_v, cell_w, table, out, joined):
    sources = table.shape[0]
    lanes = lane_iota()
    starts = segments(widths, reach)

    index = lanes
    target = lanes < 0
    from_next = lanes < 0
    for start, width in zip(starts, widths):
        early = between(lanes, start, start + reach)
        late = between(lanes, start + width - reach, start + width)
        index = jnp.where(early, lanes + width, index)
        index = jnp.where(late, lanes - width, index)
        target = target | early | late
        from_next = from_next | between(lanes, start - reach, start)
    zero = jnp.zeros((SUB, LANES), jnp.float32)
    for source in range(sources):
        after = table[source + 1] if source + 1 < sources else zero
        before = table[source - 1] if source > 0 else zero
        both = jnp.where(from_next, after, before)
        extra = jnp.take_along_axis(both, index, axis=1)
        joined[source] = table[source] + jnp.where(target, extra, 0.0)

    count = counts[0, 0]
    cells = cell_u.shape[2]
    for chunk in range(cells // LANES):
        span = slice(chunk * LANES, (chunk + 1) * LANES)
        charge = None
        for cell, start, width in zip((cell_u, cell_v, cell_w), starts, widths):
            wire = jnp.broadcast_to(cell[0, 0:1, span], (SUB, LANES))
            owner = (wire * ((1 << 18) // width + 1)) >> 18
            spot = wire - owner * width + start
            picked = zero
            for source in range(sources):
                value = jnp.take_along_axis(joined[source], spot, axis=1)
                picked = jnp.where(owner == source, value, picked)
            charge = picked if charge is None else jnp.minimum(charge, picked)
        live = lanes + chunk * LANES < count
        out[0, 0, :, span] = jnp.where(live, charge, 0.0)


def on_device(ind_frames, col_frames, ind_kernel, col_kernel, cell_u, cell_v, cell_w, tile_counts):
    reach = (ind_kernel.shape[1] - 1) // 2
    taps = ind_kernel.shape[2]
    offsets = ind_kernel.shape[1]
    ticks = ind_frames.shape[3]
    widths = (ind_frames.shape[2], ind_frames.shape[2], col_frames.shape[1])
    bins = LANES // REBIN
    tiles = ticks // REBIN // SUB
    window = taps + LANES
    blocks = ticks // LANES
    vmem = pl.BlockSpec(memory_space=pltpu.VMEM)
    outgoing = pl.pallas_call(
        lambda *refs: conv_kernel(reach, *refs),
        out_shape=jax.ShapeDtypeStruct((tiles, SUB, LANES), jnp.float32),
        in_specs=[vmem] * 4,
        out_specs=vmem,
        scratch_shapes=[
            pltpu.VMEM((48, taps), jnp.bfloat16),
            pltpu.VMEM((3, offsets * bins, 2 * window), jnp.bfloat16),
            pltpu.VMEM((3, GROUP * blocks, 2 * window), jnp.bfloat16),
        ],
        name="deconvolve",
    )(ind_frames, col_frames, ind_kernel, col_kernel)
    arrived = lax.all_to_all(outgoing, "wire", split_axis=0, concat_axis=0, tiled=True)
    return pl.pallas_call(
        lambda *refs: cell_kernel(reach, widths, *refs),
        out_shape=jax.ShapeDtypeStruct((1, 1, SUB, cell_u.shape[2]), jnp.float32),
        in_specs=[pl.BlockSpec(memory_space=pltpu.SMEM)] + [vmem] * 4,
        out_specs=vmem,
        scratch_shapes=[pltpu.VMEM((tiles, SUB, LANES), jnp.float32)],
        name="cells",
    )(tile_counts, cell_u, cell_v, cell_w, arrived)


def solution(mesh):
    return jax.shard_map(
        on_device,
        mesh=mesh,
        in_specs=(
            P("apa", None, "wire", None),
            P("apa", "wire", None),
            P(),
            P(),
            P("apa", "wire", None),
            P("apa", "wire", None),
            P("apa", "wire", None),
            P("apa", "wire"),
        ),
        out_specs=P("apa", "wire", None, None),
        check_vma=False,
    )
```

```python
import jax
import jax.numpy as jnp
from jax import lax
from jax.experimental import pallas as pl
from jax.experimental.pallas import tpu as pltpu
from jax.sharding import PartitionSpec as P

LANES = 128
SUB = 8
REBIN = 4
GROUP = 32


def lane_iota(shape=(SUB, LANES)):
    return lax.broadcasted_iota(jnp.int32, shape, 1)


def between(lanes, low, high):
    return (lanes >= low) & (lanes < high)


def segments(widths, reach):
    starts, at = [], 0
    for width in widths:
        starts.append(at + reach)
        at += width + 2 * reach
    return starts


def conv_kernel(reach, widths, ind_hbm, col_hbm, indk_hbm, colk_hbm, out, indf, colf, indk, colk, sems, toep, wide):
    copies = [pltpu.make_async_copy(source, target, sems.at[i]) for i, (source, target) in enumerate(
        ((indk_hbm, indk), (colk_hbm, colk), (ind_hbm, indf), (col_hbm, colf)))]
    for copy in copies:
        copy.start()
    offsets, taps = colk.shape
    ticks = colf.shape[2]
    window = taps + LANES
    blocks = ticks // LANES
    history = taps // LANES
    bins = LANES // REBIN

    total = (lax.broadcasted_iota(jnp.int32, (LANES, window), 0)
             + lax.broadcasted_iota(jnp.int32, (LANES, window), 1))
    fold = [between(total + LANES * i, taps, taps + REBIN).astype(jnp.float32).astype(jnp.bfloat16)
            for i in range(history)]
    fold = jnp.concatenate(fold, axis=0)
    copies[0].wait()
    copies[1].wait()
    both = indk[...]
    rows_of = [jnp.dot(k, fold, preferred_element_type=jnp.float32)
               for k in (both[:, 0, :], both[:, 1, :], colk[...])]

    lanes = lane_iota()
    subs = lax.broadcasted_iota(jnp.int32, (SUB, LANES), 0)
    pieces = window // LANES
    starts = segments(widths, reach)

    sums = []
    for plane in range(3):
        for offset in range(offsets):
            rows, at = rows_of[plane], offset
            flat = [jnp.broadcast_to(rows[at:at + 1, LANES * i:LANES * (i + 1)], (SUB, LANES))
                    for i in range(pieces)]
            made = []
            for part in range(bins // SUB):
                base = part * SUB * REBIN
                turned = [pltpu.roll(piece, base, 1, stride=REBIN, stride_axis=0) for piece in flat]
                keep = lanes >= base + REBIN * subs
                before = [jnp.zeros_like(turned[0])] + turned[:-1]
                made.append([jnp.where(keep, a, b) for a, b in zip(turned, before)])
            for pair in range(0, len(made), 2):
                at_row = offset * bins + pair * SUB
                for i in range(pieces):
                    exact = jnp.concatenate([made[pair][i], made[pair + 1][i]], axis=0)
                    high = exact.astype(jnp.bfloat16)
                    low = (exact - high.astype(jnp.float32)).astype(jnp.bfloat16)
                    toep[plane, at_row:at_row + 16, LANES * i:LANES * (i + 1)] = high
                    toep[plane, at_row:at_row + 16, window + LANES * i:window + LANES * (i + 1)] = low

    copies[2].wait()
    copies[3].wait()
    height = GROUP * blocks
    place = lax.broadcasted_iota(jnp.int32, (height, indf.shape[0]), 0)
    source = lax.broadcasted_iota(jnp.int32, (height, indf.shape[0]), 1)
    wanted = ((place & (GROUP - 1)) * blocks + place // GROUP) * 2
    ordered = [jnp.dot((source == wanted + p).astype(jnp.float32).astype(jnp.bfloat16), indf[...],
                       preferred_element_type=jnp.float32).astype(jnp.bfloat16) for p in range(2)]

    for plane in range(3):
        width = widths[plane]
        blank = jnp.zeros((GROUP, LANES), jnp.bfloat16)
        if plane < 2:
            tiles = [ordered[plane][GROUP * i:GROUP * (i + 1)] for i in range(blocks)]
        else:
            spare = jnp.zeros((GROUP - width, ticks), jnp.bfloat16)
            padded = jnp.concatenate([colf[0], spare], axis=0)
            tiles = [padded[:, LANES * i:LANES * (i + 1)] for i in range(blocks)]
        tiles = [blank] * history + tiles
        for block in range(blocks):
            for i in range(pieces):
                piece = tiles[block + i]
                wide[plane, GROUP * block:GROUP * (block + 1), LANES * i:LANES * (i + 1)] = piece
                wide[plane, GROUP * block:GROUP * (block + 1), window + LANES * i:window + LANES * (i + 1)] = piece
        grid = lax.dot_general(
            toep[plane], wide[plane], (((1,), (1,)), ((), ())),
            preferred_element_type=jnp.float32)
        sums.append(grid)

    per_half = LANES // GROUP
    for half in range(blocks // per_half):
        for part in range(bins // SUB):
            gathered = []
            for plane in range(3):
                width = widths[plane]

                def moved(shift):
                    at_row = (reach - shift) * bins + part * SUB
                    piece = sums[plane][at_row:at_row + SUB, LANES * half:LANES * (half + 1)]
                    return piece if shift == 0 else pltpu.roll(piece, shift % LANES, 1)

                spare = GROUP - width
                runs, shift = [], 0
                while shift <= reach:
                    last = min(reach, shift + spare if shift > 0 else spare)
                    runs.append((shift, last))
                    shift = last + 1
                shift = 1
                while shift <= reach:
                    last = min(reach, shift + spare)
                    runs.append((-last, -shift))
                    shift = last + 1
                for first, last in runs:
                    acc = moved(first)
                    for step in range(first + 1, last + 1):
                        acc = acc + moved(step)
                    gathered.append((plane, first, last + width, acc))
            for spot in range(per_half):
                tile = (half * per_half + spot) * (bins // SUB) + part
                result = jnp.zeros((SUB, LANES), jnp.float32)
                for plane, first, end, acc in gathered:
                    start = starts[plane]
                    placed = pltpu.roll(acc, (start - GROUP * spot) % LANES, 1)
                    valid = between(lanes, start + first, start + end)
                    result = result + jnp.where(valid, placed, 0.0)
                out[tile] = result


def cell_kernel(reach, widths, counts, cell_u, cell_v, cell_w, table, out, joined):
    sources = table.shape[0]
    lanes = lane_iota()
    starts = segments(widths, reach)

    index = lanes
    target = lanes < 0
    from_next = lanes < 0
    for start, width in zip(starts, widths):
        early = between(lanes, start, start + reach)
        late = between(lanes, start + width - reach, start + width)
        index = jnp.where(early, lanes + width, index)
        index = jnp.where(late, lanes - width, index)
        target = target | early | late
        from_next = from_next | between(lanes, start - reach, start)
    zero = jnp.zeros((SUB, LANES), jnp.float32)
    for source in range(sources):
        after = table[source + 1] if source + 1 < sources else zero
        before = table[source - 1] if source > 0 else zero
        both = jnp.where(from_next, after, before)
        extra = jnp.take_along_axis(both, index, axis=1)
        joined[source] = table[source] + jnp.where(target, extra, 0.0)

    count = counts[0, 0]
    cells = cell_u.shape[2]
    for chunk in range(cells // LANES):
        span = slice(chunk * LANES, (chunk + 1) * LANES)
        charge = None
        for cell, start, width in zip((cell_u, cell_v, cell_w), starts, widths):
            wire = jnp.broadcast_to(cell[0, 0:1, span], (SUB, LANES))
            owner = (wire * ((1 << 18) // width + 1)) >> 18
            spot = wire - owner * width + start
            picked = zero
            for source in range(sources):
                value = jnp.take_along_axis(joined[source], spot, axis=1)
                picked = jnp.where(owner == source, value, picked)
            charge = picked if charge is None else jnp.minimum(charge, picked)
        live = lanes + chunk * LANES < count
        out[0, 0, :, span] = jnp.where(live, charge, 0.0)


def on_device(ind_frames, col_frames, ind_kernel, col_kernel, cell_u, cell_v, cell_w, tile_counts):
    reach = (ind_kernel.shape[1] - 1) // 2
    taps = ind_kernel.shape[2]
    offsets = ind_kernel.shape[1]
    ticks = ind_frames.shape[3]
    widths = (ind_frames.shape[2], ind_frames.shape[2], col_frames.shape[1])
    bins = LANES // REBIN
    tiles = ticks // REBIN // SUB
    window = taps + LANES
    blocks = ticks // LANES
    vmem = pl.BlockSpec(memory_space=pltpu.VMEM)
    ind_rows = ind_frames.reshape(2, widths[0], blocks, LANES).transpose(1, 2, 0, 3).reshape(-1, LANES)
    ind_taps = ind_kernel.transpose(1, 0, 2)
    outgoing = pl.pallas_call(
        lambda *refs: conv_kernel(reach, widths, *refs),
        out_shape=jax.ShapeDtypeStruct((tiles, SUB, LANES), jnp.float32),
        in_specs=[pl.BlockSpec(memory_space=pl.ANY)] * 4,
        out_specs=vmem,
        scratch_shapes=[
            pltpu.VMEM(ind_rows.shape, jnp.bfloat16),
            pltpu.VMEM(col_frames.shape, jnp.bfloat16),
            pltpu.VMEM(ind_taps.shape, jnp.bfloat16),
            pltpu.VMEM(col_kernel.shape, jnp.bfloat16),
            pltpu.SemaphoreType.DMA((4,)),
            pltpu.VMEM((3, offsets * bins, 2 * window), jnp.bfloat16),
            pltpu.VMEM((3, GROUP * blocks, 2 * window), jnp.bfloat16),
        ],
        name="deconvolve",
    )(ind_rows, col_frames, ind_taps, col_kernel)
    arrived = lax.all_to_all(outgoing, "wire", split_axis=0, concat_axis=0, tiled=True)
    return pl.pallas_call(
        lambda *refs: cell_kernel(reach, widths, *refs),
        out_shape=jax.ShapeDtypeStruct((1, 1, SUB, cell_u.shape[2]), jnp.float32),
        in_specs=[pl.BlockSpec(memory_space=pltpu.SMEM)] + [vmem] * 4,
        out_specs=vmem,
        scratch_shapes=[pltpu.VMEM((tiles, SUB, LANES), jnp.float32)],
        name="cells",
        compiler_params=pltpu.CompilerParams(vmem_limit_bytes=4 << 20),
    )(tile_counts, cell_u, cell_v, cell_w, arrived)


def solution(mesh):
    return jax.shard_map(
        on_device,
        mesh=mesh,
        in_specs=(
            P("apa", None, "wire", None),
            P("apa", "wire", None),
            P(),
            P(),
            P("apa", "wire", None),
            P("apa", "wire", None),
            P("apa", "wire", None),
            P("apa", "wire"),
        ),
        out_specs=P("apa", "wire", None, None),
        check_vma=False,
    )
```

```python
import jax
import jax.numpy as jnp
from jax import lax
from jax.experimental import pallas as pl
from jax.experimental.pallas import tpu as pltpu
from jax.sharding import PartitionSpec as P

LANES = 128
SUB = 8
REBIN = 4
GROUP = 32
TURN = LANES // GROUP
RIGHT = 0
LEFT = 16


def lane_iota():
    return lax.broadcasted_iota(jnp.int32, (SUB, LANES), 1)


def between(lanes, low, high):
    return (lanes >= low) & (lanes < high)


def conv_kernel(reach, widths, ind_hbm, col_hbm, indk_hbm, colk_hbm, u_hbm, v_hbm, w_hbm, count_hbm,
                out, where_out, indf, colf, indk, colk, cells, count, sems, toep, wide):
    copies = [pltpu.make_async_copy(source, target, sems.at[i]) for i, (source, target) in enumerate((
        (indk_hbm, indk), (colk_hbm, colk), (ind_hbm, indf), (col_hbm, colf),
        (u_hbm, cells.at[0]), (v_hbm, cells.at[1]), (w_hbm, cells.at[2]), (count_hbm, count)))]
    for copy in copies:
        copy.start()
    offsets, taps = colk.shape
    ticks = colf.shape[2]
    window = taps + LANES
    blocks = ticks // LANES
    history = taps // LANES
    bins = LANES // REBIN
    pieces = window // LANES
    lanes = lane_iota()
    subs = lax.broadcasted_iota(jnp.int32, (SUB, LANES), 0)

    total = (lax.broadcasted_iota(jnp.int32, (taps, window), 0)
             + lax.broadcasted_iota(jnp.int32, (taps, window), 1))
    fold = between(total, taps, taps + REBIN).astype(jnp.float32).astype(jnp.bfloat16)
    height = GROUP * blocks
    place = lax.broadcasted_iota(jnp.int32, (height, indf.shape[0]), 0)
    source = lax.broadcasted_iota(jnp.int32, (height, indf.shape[0]), 1)
    wanted = ((place & (GROUP - 1)) * blocks + place // GROUP) * 2
    pick = [(source == wanted + p).astype(jnp.float32).astype(jnp.bfloat16) for p in range(2)]

    for copy in copies:
        copy.wait()

    both = indk[...]
    rows_of = [jnp.dot(k, fold, preferred_element_type=jnp.float32)
               for k in (both[:, 0, :], both[:, 1, :], colk[...])]

    sums = []
    for plane in range(3):
        width = widths[plane]
        blank = jnp.zeros((GROUP, LANES), jnp.bfloat16)
        if plane < 2:
            ordered = jnp.dot(pick[plane], indf[...], preferred_element_type=jnp.float32).astype(jnp.bfloat16)
            tiles = [ordered[GROUP * i:GROUP * (i + 1)] for i in range(blocks)]
        else:
            spare = jnp.zeros((GROUP - width, ticks), jnp.bfloat16)
            padded = jnp.concatenate([colf[0], spare], axis=0)
            tiles = [padded[:, LANES * i:LANES * (i + 1)] for i in range(blocks)]
        tiles = [blank] * history + tiles
        for block in range(blocks):
            for i in range(pieces):
                piece = tiles[block + i]
                wide[plane, GROUP * block:GROUP * (block + 1), LANES * i:LANES * (i + 1)] = piece
                wide[plane, GROUP * block:GROUP * (block + 1), window + LANES * i:window + LANES * (i + 1)] = piece
        for offset in range(offsets):
            row = rows_of[plane][offset:offset + 1, :]
            flat = [jnp.broadcast_to(row[:, LANES * i:LANES * (i + 1)], (SUB, LANES)) for i in range(pieces)]
            made = []
            for part in range(bins // SUB):
                base = part * SUB * REBIN
                turned = [pltpu.roll(piece, base, 1, stride=REBIN, stride_axis=0) for piece in flat]
                keep = lanes >= base + REBIN * subs
                before = [jnp.zeros_like(turned[0])] + turned[:-1]
                made.append([jnp.where(keep, a, b) for a, b in zip(turned, before)])
            for pair in range(0, len(made), 2):
                at_row = offset * bins + pair * SUB
                for i in range(pieces):
                    exact = jnp.concatenate([made[pair][i], made[pair + 1][i]], axis=0)
                    high = exact.astype(jnp.bfloat16)
                    low = (exact - high.astype(jnp.float32)).astype(jnp.bfloat16)
                    toep[plane, at_row:at_row + 16, LANES * i:LANES * (i + 1)] = high
                    toep[plane, at_row:at_row + 16, window + LANES * i:window + LANES * (i + 1)] = low
        grid = lax.dot_general(
            toep[plane], wide[plane], (((1,), (1,)), ((), ())),
            preferred_element_type=jnp.float32)
        sums.append(grid)

    for plane in range(3):
        width = widths[plane]
        for chunk in range(cells.shape[3] // LANES):
            span = slice(chunk * LANES, (chunk + 1) * LANES)
            wire = jnp.broadcast_to(cells[plane, 0, 0:1, span], (SUB, LANES))
            owner = (wire * ((1 << 18) // width + 1)) >> 18
            spot = wire - owner * width + ((owner + plane) & (TURN - 1)) * GROUP
            spot = spot + (owner // TURN) * LANES
            live = lanes + chunk * LANES < count[0, 0]
            where_out[plane, :, span] = jnp.where(live, spot, -1)

    turn = (lax.axis_index("wire") & (TURN - 1)) * GROUP
    spots = (lanes - turn) & (LANES - 1)
    slot = lanes & (GROUP - 1)
    per_half = LANES // GROUP
    for half in range(blocks // per_half):
        for part in range(bins // SUB):
            gathered = []
            for plane in range(3):
                width = widths[plane]
                spare = GROUP - width

                def run(first, last):
                    acc = None
                    for shift in range(first, last + 1):
                        at_row = (reach - shift) * bins + part * SUB
                        piece = sums[plane][at_row:at_row + SUB, LANES * half:LANES * (half + 1)]
                        piece = piece if shift == 0 else pltpu.roll(piece, shift % LANES, 1)
                        acc = piece if acc is None else acc + piece
                    return acc

                if spare >= reach:
                    after, before = run(0, reach), run(-reach, -1)
                    main = after + before
                else:
                    near, far = run(0, spare), run(spare + 1, reach)
                    main = near + jnp.where(slot > spare, far, 0.0)
                    after = jnp.where(slot >= width, near, 0.0) + far
                    near, far = run(-spare, -1), run(-reach, -spare - 1)
                    main = main + near + jnp.where(slot < GROUP - reach, far, 0.0)
                    before = jnp.where(slot >= width, near, 0.0) + far
                extra = (TURN - 1) * GROUP + reach * plane
                gathered += [(main, 0, GROUP * plane, width),
                             (after, width, extra + RIGHT, reach),
                             (before, -reach, extra + LEFT, reach)]
            for spot in range(per_half):
                tile = (half * per_half + spot) * (bins // SUB) + part
                result = jnp.zeros((SUB, LANES), jnp.float32)
                for acc, begin, target, size in gathered:
                    amount = (turn + (target - begin - GROUP * spot) % LANES) & (LANES - 1)
                    placed = pltpu.roll(acc, amount, 1)
                    result = jnp.where(between(spots, target, target + size), placed, result)
                out[tile] = result


def cell_kernel(reach, widths, table, wanted, out):
    sources = table.shape[0]
    lanes = lane_iota()
    group = lanes // GROUP
    slot = lanes & (GROUP - 1)
    zero = jnp.zeros((SUB, LANES), jnp.float32)

    def joined(stage, plane):
        made = None
        for i in range(TURN):
            piece = table[stage * TURN + i]
            made = piece if made is None else jnp.where(group == (plane + i) % TURN, piece, made)
        return made

    stages = sources // TURN
    halos = [joined(stage, TURN - 1) for stage in range(stages)]
    early = (group == TURN - 2) & (slot < LEFT)
    late = (group == TURN - 1) & (slot >= LEFT)
    mixed = []
    for stage in range(stages):
        made = jnp.where(early, halos[stage - 1] if stage > 0 else zero, halos[stage])
        mixed.append(jnp.where(late, halos[stage + 1] if stage + 1 < stages else zero, made))
    full = []
    for plane in range(3):
        width = widths[plane]
        first = slot < reach
        last = between(slot, width - reach, width)
        index = jnp.where(
            first, ((group - plane + 2) & (TURN - 1)) * GROUP + RIGHT + reach * plane + slot,
            ((group - plane) & (TURN - 1)) * GROUP + LEFT + reach * plane + slot - (width - reach))
        index = jnp.where(first | last, index, lanes)
        full.append([joined(stage, plane) + jnp.where(
            first | last, jnp.take_along_axis(mixed[stage], index, axis=1), 0.0) for stage in range(stages)])

    for chunk in range(wanted.shape[2] // LANES):
        span = slice(chunk * LANES, (chunk + 1) * LANES)
        charge = None
        for plane in range(3):
            at = wanted[plane, :, span]
            stage_of, lane_of = at >> 7, at & (LANES - 1)
            picked = zero
            for stage in range(stages):
                value = jnp.take_along_axis(full[plane][stage], lane_of, axis=1)
                picked = jnp.where(stage_of == stage, value, picked)
            charge = picked if charge is None else jnp.minimum(charge, picked)
        out[0, 0, :, span] = charge


def on_device(ind_frames, col_frames, ind_kernel, col_kernel, cell_u, cell_v, cell_w, tile_counts):
    offsets, taps = col_kernel.shape
    reach = (offsets - 1) // 2
    ticks = ind_frames.shape[3]
    widths = (ind_frames.shape[2], ind_frames.shape[2], col_frames.shape[1])
    bins = LANES // REBIN
    tiles = ticks // REBIN // SUB
    window = taps + LANES
    blocks = ticks // LANES
    ind_rows = ind_frames.reshape(2, widths[0], blocks, LANES).transpose(1, 2, 0, 3).reshape(-1, LANES)
    ind_taps = ind_kernel.transpose(1, 0, 2)
    vmem = pl.BlockSpec(memory_space=pltpu.VMEM)
    outgoing, wanted = pl.pallas_call(
        lambda *refs: conv_kernel(reach, widths, *refs),
        out_shape=(pltpu.VMEM((tiles, SUB, LANES), jnp.float32),
                   pltpu.VMEM((3, SUB, cell_u.shape[2]), jnp.int32)),
        in_specs=[pl.BlockSpec(memory_space=pltpu.HBM)] * 8,
        out_specs=(vmem, vmem),
        scratch_shapes=[
            pltpu.VMEM(ind_rows.shape, jnp.bfloat16),
            pltpu.VMEM(col_frames.shape, jnp.bfloat16),
            pltpu.VMEM(ind_taps.shape, jnp.bfloat16),
            pltpu.VMEM(col_kernel.shape, jnp.bfloat16),
            pltpu.VMEM((3,) + cell_u.shape[0:], jnp.int32),
            pltpu.SMEM(tile_counts.shape, jnp.int32),
            pltpu.SemaphoreType.DMA((8,)),
            pltpu.VMEM((3, offsets * bins, 2 * window), jnp.bfloat16),
            pltpu.VMEM((3, GROUP * blocks, 2 * window), jnp.bfloat16),
        ],
        name="deconvolve",
    )(ind_rows, col_frames, ind_taps, col_kernel, cell_u, cell_v, cell_w, tile_counts)
    arrived = lax.all_to_all(outgoing, "wire", split_axis=0, concat_axis=0, tiled=True)
    return pl.pallas_call(
        lambda *refs: cell_kernel(reach, widths, *refs),
        out_shape=jax.ShapeDtypeStruct((1, 1, SUB, cell_u.shape[2]), jnp.float32),
        in_specs=[vmem] * 2,
        out_specs=vmem,
        name="cells",
        compiler_params=pltpu.CompilerParams(vmem_limit_bytes=4 << 20),
    )(arrived, wanted)


def solution(mesh):
    return jax.shard_map(
        on_device,
        mesh=mesh,
        in_specs=(
            P("apa", None, "wire", None),
            P("apa", "wire", None),
            P(),
            P(),
            P("apa", "wire", None),
            P("apa", "wire", None),
            P("apa", "wire", None),
            P("apa", "wire"),
        ),
        out_specs=P("apa", "wire", None, None),
        check_vma=False,
    )
```

```python
import jax
import jax.numpy as jnp
from jax import lax
from jax.experimental import pallas as pl
from jax.experimental.pallas import tpu as pltpu
from jax.sharding import PartitionSpec as P

LANES = 128
SUB = 8
REBIN = 4
GROUP = 32
TURN = LANES // GROUP
RIGHT = 0
LEFT = 16


def lane_iota():
    return lax.broadcasted_iota(jnp.int32, (SUB, LANES), 1)


def between(lanes, low, high):
    return (lanes >= low) & (lanes < high)


def conv_kernel(reach, widths, ind_hbm, col_hbm, indk_hbm, colk_hbm, u_hbm, v_hbm, w_hbm, count_hbm,
                out, where_out, indf, colf, indk, colk, cells, count, sems, toep, wide, moved):
    copies = [pltpu.make_async_copy(source, target, sems.at[i]) for i, (source, target) in enumerate((
        (indk_hbm, indk), (colk_hbm, colk), (ind_hbm, indf), (col_hbm, colf),
        (u_hbm, cells.at[0]), (v_hbm, cells.at[1]), (w_hbm, cells.at[2]), (count_hbm, count)))]
    for copy in copies:
        copy.start()
    offsets, taps = colk.shape
    ticks = colf.shape[2]
    window = taps + LANES
    blocks = ticks // LANES
    history = taps // LANES
    bins = LANES // REBIN
    pieces = window // LANES
    lanes = lane_iota()
    subs = lax.broadcasted_iota(jnp.int32, (SUB, LANES), 0)

    total = (lax.broadcasted_iota(jnp.int32, (taps, window), 0)
             + lax.broadcasted_iota(jnp.int32, (taps, window), 1))
    fold = between(total, taps, taps + REBIN).astype(jnp.float32).astype(jnp.bfloat16)
    height = GROUP * blocks
    place = lax.broadcasted_iota(jnp.int32, (height, indf.shape[0]), 0)
    source = lax.broadcasted_iota(jnp.int32, (height, indf.shape[0]), 1)
    wanted = ((place & (GROUP - 1)) * blocks + place // GROUP) * 2
    pick = [(source == wanted + p).astype(jnp.float32).astype(jnp.bfloat16) for p in range(2)]

    copies[0].wait()
    copies[1].wait()

    both = indk[...]
    rows_of = [jnp.dot(k, fold, preferred_element_type=jnp.float32)
               for k in (both[:, 0, :], both[:, 1, :], colk[...])]

    mine = lax.axis_index("wire") & (TURN - 1)
    group = (lanes // GROUP - mine) & (TURN - 1)
    in_group = [group == i for i in range(TURN)]
    slot = lanes & (GROUP - 1)
    per_half = LANES // GROUP

    def spread(plane):
        width = widths[plane]
        blank = jnp.zeros((GROUP, LANES), jnp.bfloat16)
        if plane < 2:
            ordered = jnp.dot(pick[plane], indf[...], preferred_element_type=jnp.float32).astype(jnp.bfloat16)
            tiles = [ordered[GROUP * i:GROUP * (i + 1)] for i in range(blocks)]
        else:
            spare = jnp.zeros((GROUP - width, ticks), jnp.bfloat16)
            padded = jnp.concatenate([colf[0], spare], axis=0)
            tiles = [padded[:, LANES * i:LANES * (i + 1)] for i in range(blocks)]
        tiles = [blank] * history + tiles
        for block in range(blocks):
            for i in range(pieces):
                piece = tiles[block + i]
                wide[plane, GROUP * block:GROUP * (block + 1), LANES * i:LANES * (i + 1)] = piece
                wide[plane, GROUP * block:GROUP * (block + 1), window + LANES * i:window + LANES * (i + 1)] = piece

    def toeplitz(plane):
        for offset in range(offsets):
            row = rows_of[plane][offset:offset + 1, :]
            flat = [jnp.broadcast_to(row[:, LANES * i:LANES * (i + 1)], (SUB, LANES)) for i in range(pieces)]
            made = []
            for part in range(bins // SUB):
                base = part * SUB * REBIN
                turned = [pltpu.roll(piece, base, 1, stride=REBIN, stride_axis=0) for piece in flat]
                keep = lanes >= base + REBIN * subs
                before = [jnp.zeros_like(turned[0])] + turned[:-1]
                made.append([jnp.where(keep, a, b) for a, b in zip(turned, before)])
            for pair in range(0, len(made), 2):
                at_row = offset * bins + pair * SUB
                for i in range(pieces):
                    exact = jnp.concatenate([made[pair][i], made[pair + 1][i]], axis=0)
                    high = exact.astype(jnp.bfloat16)
                    low = (exact - high.astype(jnp.float32)).astype(jnp.bfloat16)
                    toep[plane, at_row:at_row + 16, LANES * i:LANES * (i + 1)] = high
                    toep[plane, at_row:at_row + 16, window + LANES * i:window + LANES * (i + 1)] = low

    def multiply(plane):
        grid = lax.dot_general(
            toep[plane], wide[plane], (((1,), (1,)), ((), ())),
            preferred_element_type=jnp.float32)
        return grid


    def shift_add(plane, grid):
        for half in range(blocks // per_half):
            for part in range(bins // SUB):
                width = widths[plane]
                spare = GROUP - width

                def run(first, last):
                    acc = None
                    for shift in range(first, last + 1):
                        at_row = (reach - shift) * bins + part * SUB
                        piece = grid[at_row:at_row + SUB, LANES * half:LANES * (half + 1)]
                        piece = piece if shift == 0 else pltpu.roll(piece, shift % LANES, 1)
                        acc = piece if acc is None else acc + piece
                    return acc

                if spare >= reach:
                    after, before = run(0, reach), run(-reach, -1)
                    main = after + before
                else:
                    near, far = run(0, spare), run(spare + 1, reach)
                    main = near + jnp.where(slot > spare, far, 0.0)
                    after = jnp.where(slot >= width, near, 0.0) + far
                    near, far = run(-spare, -1), run(-reach, -spare - 1)
                    main = main + near + jnp.where(slot < GROUP - reach, far, 0.0)
                    before = jnp.where(slot >= width, near, 0.0) + far
                main = pltpu.roll(main, ((plane + mine) & (TURN - 1)) * GROUP, 1)
                for i, value in enumerate((main, after, before)):
                    moved[plane, i, half * (bins // SUB) + part] = value

    for copy in copies[2:]:
        copy.wait()
    grids = []
    for plane in range(3):
        spread(plane)
        toeplitz(plane)
        grids.append(multiply(plane))
    for plane in range(3):
        shift_add(plane, grids[plane])

    stand = lax.axis_index("wire") // (bins // SUB) & (TURN - 1)
    for plane in range(3):
        width = widths[plane]
        for chunk in range(cells.shape[3] // LANES):
            span = slice(chunk * LANES, (chunk + 1) * LANES)
            wire = jnp.broadcast_to(cells[plane, 0, 0:1, span], (SUB, LANES))
            owner = (wire * ((1 << 18) // width + 1)) >> 18
            spot = wire - owner * width + ((owner + plane + stand) & (TURN - 1)) * GROUP
            spot = spot + (owner // TURN) * LANES
            live = lanes + chunk * LANES < count[0, 0]
            where_out[plane, :, span] = jnp.where(live, spot, -1)


    edge = ((TURN - 1 + mine) & (TURN - 1)) * GROUP
    for half in range(blocks // per_half):
        for part in range(bins // SUB):
            step = half * (bins // SUB) + part
            turned = [moved[plane, 0, step] for plane in range(3)]
            edges, halo = [], None
            for plane in range(3):
                edges += [(RIGHT + reach * plane, widths[plane], moved[plane, 1, step]),
                          (LEFT + reach * plane, -reach, moved[plane, 2, step])]
            for target, begin, acc in sorted(edges, key=lambda item: item[0]):
                placed = pltpu.roll(acc, (edge + (target - begin) % LANES) & (LANES - 1), 1)
                halo = placed if halo is None else jnp.where(slot >= target, placed, halo)
            turned.append(halo)
            for spot in range(per_half):
                tile = (half * per_half + spot) * (bins // SUB) + part
                result = turned[0]
                for plane in range(1, TURN):
                    result = jnp.where(in_group[(spot + plane) % TURN], turned[plane], result)
                out[tile] = result


def cell_kernel(reach, widths, table, wanted, out):
    sources = table.shape[0]
    lanes = lane_iota()
    stand = lax.axis_index("wire") // (LANES // REBIN // SUB) & (TURN - 1)
    group = (lanes // GROUP - stand) & (TURN - 1)
    slot = lanes & (GROUP - 1)
    zero = jnp.zeros((SUB, LANES), jnp.float32)

    def joined(stage, plane):
        made = None
        for i in range(TURN):
            piece = table[stage * TURN + i]
            made = piece if made is None else jnp.where(group == (plane + i) % TURN, piece, made)
        return made

    stages = sources // TURN
    halos = [joined(stage, TURN - 1) for stage in range(stages)]
    early = (group == TURN - 2) & (slot < LEFT)
    late = (group == TURN - 1) & (slot >= LEFT)
    mixed = []
    for stage in range(stages):
        made = jnp.where(early, halos[stage - 1] if stage > 0 else zero, halos[stage])
        mixed.append(jnp.where(late, halos[stage + 1] if stage + 1 < stages else zero, made))
    full = []
    for plane in range(3):
        width = widths[plane]
        first = slot < reach
        last = between(slot, width - reach, width)
        index = jnp.where(
            first, ((group - plane + 2 + stand) & (TURN - 1)) * GROUP + RIGHT + reach * plane + slot,
            ((group - plane + stand) & (TURN - 1)) * GROUP + LEFT + reach * plane + slot - (width - reach))
        index = jnp.where(first | last, index, lanes)
        full.append([joined(stage, plane) + jnp.where(
            first | last, jnp.take_along_axis(mixed[stage], index, axis=1), 0.0) for stage in range(stages)])

    for chunk in range(wanted.shape[2] // LANES):
        span = slice(chunk * LANES, (chunk + 1) * LANES)
        charge = None
        for plane in range(3):
            at = wanted[plane, :, span]
            stage_of, lane_of = at >> 7, at & (LANES - 1)
            picked = zero
            for stage in range(stages):
                value = jnp.take_along_axis(full[plane][stage], lane_of, axis=1)
                picked = jnp.where(stage_of == stage, value, picked)
            charge = picked if charge is None else jnp.minimum(charge, picked)
        out[0, 0, :, span] = charge


def on_device(ind_frames, col_frames, ind_kernel, col_kernel, cell_u, cell_v, cell_w, tile_counts):
    offsets, taps = col_kernel.shape
    reach = (offsets - 1) // 2
    ticks = ind_frames.shape[3]
    widths = (ind_frames.shape[2], ind_frames.shape[2], col_frames.shape[1])
    bins = LANES // REBIN
    tiles = ticks // REBIN // SUB
    window = taps + LANES
    blocks = ticks // LANES
    ind_rows = ind_frames.reshape(2, widths[0], blocks, LANES).transpose(1, 2, 0, 3).reshape(-1, LANES)
    ind_taps = ind_kernel.transpose(1, 0, 2)
    vmem = pl.BlockSpec(memory_space=pltpu.VMEM)
    outgoing, wanted = pl.pallas_call(
        lambda *refs: conv_kernel(reach, widths, *refs),
        out_shape=(pltpu.VMEM((tiles, SUB, LANES), jnp.float32),
                   pltpu.VMEM((3, SUB, cell_u.shape[2]), jnp.int32)),
        in_specs=[pl.BlockSpec(memory_space=pltpu.HBM)] * 8,
        out_specs=(vmem, vmem),
        scratch_shapes=[
            pltpu.VMEM(ind_rows.shape, jnp.bfloat16),
            pltpu.VMEM(col_frames.shape, jnp.bfloat16),
            pltpu.VMEM(ind_taps.shape, jnp.bfloat16),
            pltpu.VMEM(col_kernel.shape, jnp.bfloat16),
            pltpu.VMEM((3,) + cell_u.shape[0:], jnp.int32),
            pltpu.SMEM(tile_counts.shape, jnp.int32),
            pltpu.SemaphoreType.DMA((8,)),
            pltpu.VMEM((3, offsets * bins, 2 * window), jnp.bfloat16),
            pltpu.VMEM((3, GROUP * blocks, 2 * window), jnp.bfloat16),
            pltpu.VMEM((3, 3, tiles // TURN, SUB, LANES), jnp.float32),
        ],
        name="deconvolve",
    )(ind_rows, col_frames, ind_taps, col_kernel, cell_u, cell_v, cell_w, tile_counts)
    arrived = lax.all_to_all(outgoing, "wire", split_axis=0, concat_axis=0, tiled=True)
    return pl.pallas_call(
        lambda *refs: cell_kernel(reach, widths, *refs),
        out_shape=jax.ShapeDtypeStruct((1, 1, SUB, cell_u.shape[2]), jnp.float32),
        in_specs=[vmem] * 2,
        out_specs=vmem,
        name="cells",
        compiler_params=pltpu.CompilerParams(vmem_limit_bytes=4 << 20),
    )(arrived, wanted)


def solution(mesh):
    return jax.shard_map(
        on_device,
        mesh=mesh,
        in_specs=(
            P("apa", None, "wire", None),
            P("apa", "wire", None),
            P(),
            P(),
            P("apa", "wire", None),
            P("apa", "wire", None),
            P("apa", "wire", None),
            P("apa", "wire"),
        ),
        out_specs=P("apa", "wire", None, None),
        check_vma=False,
    )
```

```python
import jax
import jax.numpy as jnp
from jax import lax
from jax.experimental import pallas as pl
from jax.experimental.pallas import tpu as pltpu
from jax.sharding import PartitionSpec as P

LANES = 128
SUB = 8
REBIN = 4
HALF = 16
GROUP = 32
TURN = LANES // GROUP
RIGHT = 0
LEFT = 16


def lane_iota():
    return lax.broadcasted_iota(jnp.int32, (SUB, LANES), 1)


def between(lanes, low, high):
    return (lanes >= low) & (lanes < high)


def conv_kernel(reach, widths, ind_hbm, col_hbm, indk_hbm, colk_hbm, u_hbm, v_hbm, w_hbm, count_hbm,
                out, where_out, indf, colf, indk, colk, cells, count, sems, toep, wide, moved):
    copies = [pltpu.make_async_copy(source, target, sems.at[i]) for i, (source, target) in enumerate((
        (indk_hbm, indk), (colk_hbm, colk), (ind_hbm, indf), (col_hbm, colf),
        (u_hbm, cells.at[0]), (v_hbm, cells.at[1]), (w_hbm, cells.at[2]), (count_hbm, count)))]
    for copy in copies:
        copy.start()
    offsets, taps = colk.shape
    ticks = colf.shape[2]
    window = taps + LANES
    blocks = ticks // LANES
    history = taps // LANES
    bins = LANES // REBIN
    pieces = window // LANES
    lanes = lane_iota()
    subs = lax.broadcasted_iota(jnp.int32, (SUB, LANES), 0)

    total = (lax.broadcasted_iota(jnp.int32, (taps, window), 0)
             + lax.broadcasted_iota(jnp.int32, (taps, window), 1))
    fold = between(total, taps, taps + REBIN).astype(jnp.float32).astype(jnp.bfloat16)
    part_rows = 2 * blocks * HALF
    place = lax.broadcasted_iota(jnp.int32, (part_rows, part_rows), 0)
    source = lax.broadcasted_iota(jnp.int32, (part_rows, part_rows), 1)
    wanted = (place & (HALF - 1)) * (2 * blocks) + (place // HALF & (blocks - 1)) * 2 + place // (part_rows // 2)
    pick = (source == wanted).astype(jnp.float32).astype(jnp.bfloat16)

    copies[0].wait()
    copies[1].wait()

    both = indk[...]
    rows_of = [jnp.dot(k, fold, preferred_element_type=jnp.float32)
               for k in (both[:, 0, :], both[:, 1, :], colk[...])]

    mine = lax.axis_index("wire") & (TURN - 1)
    group = (lanes // GROUP - mine) & (TURN - 1)
    in_group = [group == i for i in range(TURN)]
    slot = lanes & (GROUP - 1)
    per_half = LANES // GROUP

    def spread(plane, rows):
        width = widths[plane]
        blank = jnp.zeros((HALF, LANES), jnp.bfloat16)
        for part in range(GROUP // HALF):
            if plane < 2:
                at = plane * blocks
                tiles = [rows[part][HALF * (at + i):HALF * (at + i + 1)] for i in range(blocks)]
            else:
                count = min(HALF, width - HALF * part)
                mine = colf[0, HALF * part:HALF * part + count, :]
                if count < HALF:
                    mine = jnp.concatenate([mine, jnp.zeros((HALF - count, ticks), jnp.bfloat16)], axis=0)
                tiles = [mine[:, LANES * i:LANES * (i + 1)] for i in range(blocks)]
            for block, piece in enumerate([blank] * history + tiles):
                row = GROUP * block + HALF * part
                wide[plane, row:row + HALF, :] = piece

    def toeplitz(plane):
        for offset in range(offsets):
            row = rows_of[plane][offset:offset + 1, :]
            flat = [jnp.broadcast_to(row[:, LANES * i:LANES * (i + 1)], (SUB, LANES)) for i in range(pieces)]
            made = []
            for part in range(bins // SUB):
                base = part * SUB * REBIN
                turned = [pltpu.roll(piece, base, 1, stride=REBIN, stride_axis=0) for piece in flat]
                keep = lanes >= base + REBIN * subs
                before = [jnp.zeros_like(turned[0])] + turned[:-1]
                made.append([jnp.where(keep, a, b) for a, b in zip(turned, before)])
            for pair in range(0, len(made), 2):
                at_row = offset * bins + pair * SUB
                for i in range(pieces):
                    exact = jnp.concatenate([made[pair][i], made[pair + 1][i]], axis=0)
                    high = exact.astype(jnp.bfloat16)
                    low = (exact - high.astype(jnp.float32)).astype(jnp.bfloat16)
                    toep[plane, at_row:at_row + 16, LANES * i:LANES * (i + 1)] = high
                    toep[plane, at_row:at_row + 16, window + LANES * i:window + LANES * (i + 1)] = low

    def multiply(plane):
        seen = [wide[plane, GROUP * i:GROUP * (i + blocks), :] for i in range(pieces)]
        grid = lax.dot_general(
            toep[plane], jnp.concatenate(seen + seen, axis=1), (((1,), (1,)), ((), ())),
            preferred_element_type=jnp.float32)
        return grid


    def shift_add(plane, grid):
        for half in range(blocks // per_half):
            for part in range(bins // SUB):
                width = widths[plane]
                spare = GROUP - width

                def run(first, last):
                    acc = None
                    for shift in range(first, last + 1):
                        at_row = (reach - shift) * bins + part * SUB
                        piece = grid[at_row:at_row + SUB, LANES * half:LANES * (half + 1)]
                        piece = piece if shift == 0 else pltpu.roll(piece, shift % LANES, 1)
                        acc = piece if acc is None else acc + piece
                    return acc

                if spare >= reach:
                    after, before = run(0, reach), run(-reach, -1)
                    main = after + before
                else:
                    near, far = run(0, spare), run(spare + 1, reach)
                    main = near + jnp.where(slot > spare, far, 0.0)
                    after = jnp.where(slot >= width, near, 0.0) + far
                    near, far = run(-spare, -1), run(-reach, -spare - 1)
                    main = main + near + jnp.where(slot < GROUP - reach, far, 0.0)
                    before = jnp.where(slot >= width, near, 0.0) + far
                main = pltpu.roll(main, ((plane + mine) & (TURN - 1)) * GROUP, 1)
                for i, value in enumerate((main, after, before)):
                    moved[plane, i, half * (bins // SUB) + part] = value

    for copy in copies[2:]:
        copy.wait()
    rows = [jnp.dot(pick[:, :min(part_rows, indf.shape[0] - at)], indf[at:min(at + part_rows, indf.shape[0]), :],
                    preferred_element_type=jnp.float32).astype(jnp.bfloat16)
            for at in range(0, indf.shape[0], part_rows)]
    grids = []
    for plane in range(3):
        spread(plane, rows)
        toeplitz(plane)
    for plane in range(3):
        grids.append(multiply(plane))
    for plane in range(3):
        shift_add(plane, grids[plane])

    stand = lax.axis_index("wire") // (bins // SUB) & (TURN - 1)
    for plane in range(3):
        width = widths[plane]
        for chunk in range(cells.shape[3] // LANES):
            span = slice(chunk * LANES, (chunk + 1) * LANES)
            wire = jnp.broadcast_to(cells[plane, 0, 0:1, span], (SUB, LANES))
            owner = (wire * ((1 << 18) // width + 1)) >> 18
            spot = wire - owner * width + ((owner + plane + stand) & (TURN - 1)) * GROUP
            spot = spot + (owner // TURN) * LANES
            live = lanes + chunk * LANES < count[0, 0]
            where_out[plane, :, span] = jnp.where(live, spot, -1)


    edge = ((TURN - 1 + mine) & (TURN - 1)) * GROUP
    for half in range(blocks // per_half):
        for part in range(bins // SUB):
            step = half * (bins // SUB) + part
            turned = [moved[plane, 0, step] for plane in range(3)]
            edges, halo = [], None
            for plane in range(3):
                edges += [(RIGHT + reach * plane, widths[plane], moved[plane, 1, step]),
                          (LEFT + reach * plane, -reach, moved[plane, 2, step])]
            for target, begin, acc in sorted(edges, key=lambda item: item[0]):
                placed = pltpu.roll(acc, (edge + (target - begin) % LANES) & (LANES - 1), 1)
                halo = placed if halo is None else jnp.where(slot >= target, placed, halo)
            turned.append(halo)
            for spot in range(per_half):
                tile = (half * per_half + spot) * (bins // SUB) + part
                result = turned[0]
                for plane in range(1, TURN):
                    result = jnp.where(in_group[(spot + plane) % TURN], turned[plane], result)
                out[tile] = result


def cell_kernel(reach, widths, table, wanted, out):
    sources = table.shape[0]
    lanes = lane_iota()
    stand = lax.axis_index("wire") // (LANES // REBIN // SUB) & (TURN - 1)
    group = (lanes // GROUP - stand) & (TURN - 1)
    slot = lanes & (GROUP - 1)
    zero = jnp.zeros((SUB, LANES), jnp.float32)

    def joined(stage, plane):
        made = None
        for i in range(TURN):
            piece = table[stage * TURN + i]
            made = piece if made is None else jnp.where(group == (plane + i) % TURN, piece, made)
        return made

    stages = sources // TURN
    halos = [joined(stage, TURN - 1) for stage in range(stages)]
    early = (group == TURN - 2) & (slot < LEFT)
    late = (group == TURN - 1) & (slot >= LEFT)
    mixed = []
    for stage in range(stages):
        made = jnp.where(early, halos[stage - 1] if stage > 0 else zero, halos[stage])
        mixed.append(jnp.where(late, halos[stage + 1] if stage + 1 < stages else zero, made))
    full = []
    for plane in range(3):
        width = widths[plane]
        first = slot < reach
        last = between(slot, width - reach, width)
        index = jnp.where(
            first, ((group - plane + 2 + stand) & (TURN - 1)) * GROUP + RIGHT + reach * plane + slot,
            ((group - plane + stand) & (TURN - 1)) * GROUP + LEFT + reach * plane + slot - (width - reach))
        index = jnp.where(first | last, index, lanes)
        full.append([joined(stage, plane) + jnp.where(
            first | last, jnp.take_along_axis(mixed[stage], index, axis=1), 0.0) for stage in range(stages)])

    for chunk in range(wanted.shape[2] // LANES):
        span = slice(chunk * LANES, (chunk + 1) * LANES)
        charge = None
        for plane in range(3):
            at = wanted[plane, :, span]
            stage_of, lane_of = at >> 7, at & (LANES - 1)
            picked = zero
            for stage in range(stages):
                value = jnp.take_along_axis(full[plane][stage], lane_of, axis=1)
                picked = jnp.where(stage_of == stage, value, picked)
            charge = picked if charge is None else jnp.minimum(charge, picked)
        out[0, 0, :, span] = charge


def on_device(ind_frames, col_frames, ind_kernel, col_kernel, cell_u, cell_v, cell_w, tile_counts):
    offsets, taps = col_kernel.shape
    reach = (offsets - 1) // 2
    ticks = ind_frames.shape[3]
    widths = (ind_frames.shape[2], ind_frames.shape[2], col_frames.shape[1])
    bins = LANES // REBIN
    tiles = ticks // REBIN // SUB
    window = taps + LANES
    blocks = ticks // LANES
    ind_rows = ind_frames.reshape(2, widths[0], blocks, LANES).transpose(1, 2, 0, 3).reshape(-1, LANES)
    ind_taps = ind_kernel.transpose(1, 0, 2)
    vmem = pl.BlockSpec(memory_space=pltpu.VMEM)
    outgoing, wanted = pl.pallas_call(
        lambda *refs: conv_kernel(reach, widths, *refs),
        out_shape=(pltpu.VMEM((tiles, SUB, LANES), jnp.float32),
                   pltpu.VMEM((3, SUB, cell_u.shape[2]), jnp.int32)),
        in_specs=[pl.BlockSpec(memory_space=pltpu.HBM)] * 8,
        out_specs=(vmem, vmem),
        scratch_shapes=[
            pltpu.VMEM(ind_rows.shape, jnp.bfloat16),
            pltpu.VMEM(col_frames.shape, jnp.bfloat16),
            pltpu.VMEM(ind_taps.shape, jnp.bfloat16),
            pltpu.VMEM(col_kernel.shape, jnp.bfloat16),
            pltpu.VMEM((3,) + cell_u.shape[0:], jnp.int32),
            pltpu.SMEM(tile_counts.shape, jnp.int32),
            pltpu.SemaphoreType.DMA((8,)),
            pltpu.VMEM((3, offsets * bins, 2 * window), jnp.bfloat16),
            pltpu.VMEM((3, GROUP * (blocks + taps // LANES), LANES), jnp.bfloat16),
            pltpu.VMEM((3, 3, tiles // TURN, SUB, LANES), jnp.float32),
        ],
        name="deconvolve",
    )(ind_rows, col_frames, ind_taps, col_kernel, cell_u, cell_v, cell_w, tile_counts)
    arrived = lax.all_to_all(outgoing, "wire", split_axis=0, concat_axis=0, tiled=True)
    return pl.pallas_call(
        lambda *refs: cell_kernel(reach, widths, *refs),
        out_shape=jax.ShapeDtypeStruct((1, 1, SUB, cell_u.shape[2]), jnp.float32),
        in_specs=[vmem] * 2,
        out_specs=vmem,
        name="cells",
        compiler_params=pltpu.CompilerParams(vmem_limit_bytes=4 << 20),
    )(arrived, wanted)


def solution(mesh):
    return jax.shard_map(
        on_device,
        mesh=mesh,
        in_specs=(
            P("apa", None, "wire", None),
            P("apa", "wire", None),
            P(),
            P(),
            P("apa", "wire", None),
            P("apa", "wire", None),
            P("apa", "wire", None),
            P("apa", "wire"),
        ),
        out_specs=P("apa", "wire", None, None),
        check_vma=False,
    )
```

```python
import jax
import jax.numpy as jnp
from jax import lax
from jax.experimental import pallas as pl
from jax.experimental.pallas import tpu as pltpu
from jax.sharding import PartitionSpec as P

LANES = 128
SUB = 8
REBIN = 4
HALF = 16
GROUP = 32
TURN = LANES // GROUP
RIGHT = 0
LEFT = 16


def lane_iota():
    return lax.broadcasted_iota(jnp.int32, (SUB, LANES), 1)


def between(lanes, low, high):
    return (lanes >= low) & (lanes < high)


def conv_kernel(reach, widths, ind_hbm, col_hbm, indk_hbm, colk_hbm, u_hbm, v_hbm, w_hbm, count_hbm,
                out, where_out, extras, indf, colf, indk, colk, cells, count, sems, toep, wide, filters, moved):
    copies = [pltpu.make_async_copy(source, target, sems.at[i]) for i, (source, target) in enumerate((
        (indk_hbm, indk), (colk_hbm, colk), (ind_hbm.at[0:256], indf.at[0:256]), (ind_hbm.at[256:400], indf.at[256:400]), (col_hbm.at[:, :, 0:512], colf.at[:, :, 0:512]), (col_hbm.at[:, :, 512:1024], colf.at[:, :, 512:1024]),
        (u_hbm, cells.at[0]), (v_hbm, cells.at[1]), (w_hbm, cells.at[2]), (count_hbm, count)))]
    for copy in copies:
        copy.start()
    offsets, taps = colk.shape
    ticks = colf.shape[2]
    window = taps + LANES
    blocks = ticks // LANES
    history = taps // LANES
    bins = LANES // REBIN
    pieces = window // LANES
    lanes = lane_iota()
    subs = lax.broadcasted_iota(jnp.int32, (SUB, LANES), 0)

    tap = lax.broadcasted_iota(jnp.int32, (taps, window), 0)
    column = lax.broadcasted_iota(jnp.int32, (taps, window), 1)
    total = tap + jnp.where(column < taps, column, taps + (column & (REBIN - 1)))
    fold = between(total, taps, taps + REBIN).astype(jnp.float32).astype(jnp.bfloat16)
    part_rows = 2 * blocks * HALF
    place = lax.broadcasted_iota(jnp.int32, (part_rows, part_rows), 0)
    source = lax.broadcasted_iota(jnp.int32, (part_rows, part_rows), 1)
    wanted = (place & (HALF - 1)) * (2 * blocks) + (place // HALF & (blocks - 1)) * 2 + place // (part_rows // 2)
    pick = (source == wanted).astype(jnp.float32).astype(jnp.bfloat16)

    stand = lax.axis_index("wire") // (bins // SUB) & (TURN - 1)
    group = (lanes // GROUP - stand) & (TURN - 1)
    slot = lanes & (GROUP - 1)
    for plane in range(3):
        width = widths[plane]
        first = slot < reach
        last = between(slot, width - reach, width)
        index = jnp.where(
            first, ((group - plane + 2 + stand) & (TURN - 1)) * GROUP + RIGHT + reach * plane + slot,
            ((group - plane + stand) & (TURN - 1)) * GROUP + LEFT + reach * plane + slot - (width - reach))
        extras[plane] = jnp.where(first | last, index, -1)

    filters[...] = jnp.zeros_like(filters)
    copies[0].wait()
    copies[1].wait()

    both = indk[...]
    for plane, k in enumerate((both[:, 0, :], both[:, 1, :], colk[...])):
        filters[16 * plane:16 * plane + offsets, :] = k
    all_rows = jnp.dot(filters[...], fold, preferred_element_type=jnp.float32)
    rows_of = [all_rows[16 * plane:16 * plane + offsets] for plane in range(3)]

    mine = lax.axis_index("wire") & (TURN - 1)
    group = (lanes // GROUP - mine) & (TURN - 1)
    in_group = [group == i for i in range(TURN)]
    slot = lanes & (GROUP - 1)
    per_half = LANES // GROUP

    def spread(plane, rows):
        width = widths[plane]
        blank = jnp.zeros((HALF, LANES), jnp.bfloat16)
        for part in range(GROUP // HALF):
            if plane < 2:
                at = plane * blocks
                tiles = [rows[part][HALF * (at + i):HALF * (at + i + 1)] for i in range(blocks)]
            else:
                count = min(HALF, width - HALF * part)
                mine = colf[0, HALF * part:HALF * part + count, :]
                if count < HALF:
                    mine = jnp.concatenate([mine, jnp.zeros((HALF - count, ticks), jnp.bfloat16)], axis=0)
                tiles = [mine[:, LANES * i:LANES * (i + 1)] for i in range(blocks)]
            for block, piece in enumerate([blank] * history + tiles):
                row = GROUP * block + HALF * part
                wide[plane, row:row + HALF, :] = piece

    def toeplitz(plane):
        for offset in range(offsets):
            row = rows_of[plane][offset:offset + 1, :]
            flat = [jnp.broadcast_to(row[:, LANES * i:LANES * (i + 1)], (SUB, LANES)) for i in range(pieces)]
            made = []
            for part in range(bins // SUB):
                base = part * SUB * REBIN
                shift = base + REBIN * subs
                turned = [pltpu.roll(piece, base, 1, stride=REBIN, stride_axis=0) for piece in flat[:-1]]
                own = jnp.where(lanes < shift + REBIN, flat[-1], 0.0)
                after = turned[1:] + [own]
                before = turned
                made.append([jnp.where(lanes >= shift, turned[0], 0.0)]
                            + [jnp.where(lanes >= shift, a, b) for a, b in zip(after, before)])
            for pair in range(0, len(made), 2):
                at_row = offset * bins + pair * SUB
                for i in range(pieces):
                    exact = jnp.concatenate([made[pair][i], made[pair + 1][i]], axis=0)
                    high = exact.astype(jnp.bfloat16)
                    low = (exact - high.astype(jnp.float32)).astype(jnp.bfloat16)
                    toep[plane, at_row:at_row + 16, LANES * i:LANES * (i + 1)] = high
                    toep[plane, at_row:at_row + 16, window + LANES * i:window + LANES * (i + 1)] = low

    def multiply(plane):
        seen = [wide[plane, GROUP * i:GROUP * (i + blocks), :] for i in range(pieces)]
        grid = lax.dot_general(
            toep[plane], jnp.concatenate(seen + seen, axis=1), (((1,), (1,)), ((), ())),
            preferred_element_type=jnp.float32)
        return grid


    def shift_add(plane, grid):
        for half in range(blocks // per_half):
            for part in range(bins // SUB):
                width = widths[plane]
                spare = GROUP - width

                def run(first, last):
                    acc = None
                    for shift in range(first, last + 1):
                        at_row = (reach - shift) * bins + part * SUB
                        piece = grid[at_row:at_row + SUB, LANES * half:LANES * (half + 1)]
                        piece = piece if shift == 0 else pltpu.roll(piece, shift % LANES, 1)
                        acc = piece if acc is None else acc + piece
                    return acc

                if spare >= reach:
                    after, before = run(0, reach), run(-reach, -1)
                    main = after + before
                else:
                    near, far = run(0, spare), run(spare + 1, reach)
                    main = near + jnp.where(slot > spare, far, 0.0)
                    after = jnp.where(slot >= width, near, 0.0) + far
                    near, far = run(-spare, -1), run(-reach, -spare - 1)
                    main = main + near + jnp.where(slot < GROUP - reach, far, 0.0)
                    before = jnp.where(slot >= width, near, 0.0) + far
                main = pltpu.roll(main, ((plane + mine) & (TURN - 1)) * GROUP, 1)
                for i, value in enumerate((main, after, before)):
                    moved[plane, i, half * (bins // SUB) + part] = value

    for copy in copies[2:]:
        copy.wait()
    rows = [jnp.dot(pick[:, :min(part_rows, indf.shape[0] - at)], indf[at:min(at + part_rows, indf.shape[0]), :],
                    preferred_element_type=jnp.float32).astype(jnp.bfloat16)
            for at in range(0, indf.shape[0], part_rows)]
    grids = []
    for plane in range(3):
        spread(plane, rows)
        toeplitz(plane)
    for plane in range(3):
        grids.append(multiply(plane))
    for plane in range(3):
        shift_add(plane, grids[plane])

    stand = lax.axis_index("wire") // (bins // SUB) & (TURN - 1)
    for plane in range(3):
        width = widths[plane]
        for chunk in range(cells.shape[3] // LANES):
            span = slice(chunk * LANES, (chunk + 1) * LANES)
            wire = jnp.broadcast_to(cells[plane, 0, 0:1, span], (SUB, LANES))
            owner = (wire * ((1 << 18) // width + 1)) >> 18
            spot = wire - owner * width + ((owner + plane + stand) & (TURN - 1)) * GROUP
            spot = spot + (owner // TURN) * LANES
            live = lanes + chunk * LANES < count[0, 0]
            where_out[plane, :, span] = jnp.where(live, spot, -1)


    edge = ((TURN - 1 + mine) & (TURN - 1)) * GROUP
    for half in range(blocks // per_half):
        for part in range(bins // SUB):
            step = half * (bins // SUB) + part
            turned = [moved[plane, 0, step] for plane in range(3)]
            edges, halo = [], None
            for plane in range(3):
                edges += [(RIGHT + reach * plane, widths[plane], moved[plane, 1, step]),
                          (LEFT + reach * plane, -reach, moved[plane, 2, step])]
            for target, begin, acc in sorted(edges, key=lambda item: item[0]):
                placed = pltpu.roll(acc, (edge + (target - begin) % LANES) & (LANES - 1), 1)
                halo = placed if halo is None else jnp.where(slot >= target, placed, halo)
            turned.append(halo)
            for spot in range(per_half):
                tile = (half * per_half + spot) * (bins // SUB) + part
                result = turned[0]
                for plane in range(1, TURN):
                    result = jnp.where(in_group[(spot + plane) % TURN], turned[plane], result)
                out[tile] = result


def cell_kernel(table, wanted, extras, out):
    sources = table.shape[0]
    lanes = lane_iota()
    stand = lax.axis_index("wire") // (LANES // REBIN // SUB) & (TURN - 1)
    group = (lanes // GROUP - stand) & (TURN - 1)
    slot = lanes & (GROUP - 1)
    zero = jnp.zeros((SUB, LANES), jnp.float32)

    def joined(stage, plane):
        made = None
        for i in range(TURN):
            piece = table[stage * TURN + i]
            made = piece if made is None else jnp.where(group == (plane + i) % TURN, piece, made)
        return made

    stages = sources // TURN
    halos = [joined(stage, TURN - 1) for stage in range(stages)]
    early = (group == TURN - 2) & (slot < LEFT)
    late = (group == TURN - 1) & (slot >= LEFT)
    mixed = []
    for stage in range(stages):
        made = jnp.where(early, halos[stage - 1] if stage > 0 else zero, halos[stage])
        mixed.append(jnp.where(late, halos[stage + 1] if stage + 1 < stages else zero, made))
    full = []
    for plane in range(3):
        index = extras[plane]
        added = index >= 0
        index = index & (LANES - 1)
        full.append([joined(stage, plane) + jnp.where(
            added, jnp.take_along_axis(mixed[stage], index, axis=1), 0.0) for stage in range(stages)])

    for chunk in range(wanted.shape[2] // LANES):
        span = slice(chunk * LANES, (chunk + 1) * LANES)
        charge = None
        for plane in range(3):
            at = wanted[plane, :, span]
            stage_of, lane_of = at >> 7, at & (LANES - 1)
            picked = zero
            for stage in range(stages):
                value = jnp.take_along_axis(full[plane][stage], lane_of, axis=1)
                picked = jnp.where(stage_of == stage, value, picked)
            charge = picked if charge is None else jnp.minimum(charge, picked)
        out[0, 0, :, span] = charge


def on_device(ind_frames, col_frames, ind_kernel, col_kernel, cell_u, cell_v, cell_w, tile_counts):
    offsets, taps = col_kernel.shape
    reach = (offsets - 1) // 2
    ticks = ind_frames.shape[3]
    widths = (ind_frames.shape[2], ind_frames.shape[2], col_frames.shape[1])
    bins = LANES // REBIN
    tiles = ticks // REBIN // SUB
    window = taps + LANES
    blocks = ticks // LANES
    ind_rows = ind_frames.reshape(2, widths[0], blocks, LANES).transpose(1, 2, 0, 3).reshape(-1, LANES)
    ind_taps = ind_kernel.transpose(1, 0, 2)
    vmem = pl.BlockSpec(memory_space=pltpu.VMEM)
    outgoing, wanted, extras = pl.pallas_call(
        lambda *refs: conv_kernel(reach, widths, *refs),
        out_shape=(pltpu.VMEM((tiles, SUB, LANES), jnp.float32),
                   pltpu.VMEM((3, SUB, cell_u.shape[2]), jnp.int32),
                   pltpu.VMEM((3, SUB, LANES), jnp.int32)),
        in_specs=[pl.BlockSpec(memory_space=pltpu.HBM)] * 8,
        out_specs=(vmem, vmem, vmem),
        scratch_shapes=[
            pltpu.VMEM(ind_rows.shape, jnp.bfloat16),
            pltpu.VMEM(col_frames.shape, jnp.bfloat16),
            pltpu.VMEM(ind_taps.shape, jnp.bfloat16),
            pltpu.VMEM(col_kernel.shape, jnp.bfloat16),
            pltpu.VMEM((3,) + cell_u.shape[0:], jnp.int32),
            pltpu.SMEM(tile_counts.shape, jnp.int32),
            pltpu.SemaphoreType.DMA((10,)),
            pltpu.VMEM((3, offsets * bins, 2 * window), jnp.bfloat16),
            pltpu.VMEM((3, GROUP * (blocks + taps // LANES), LANES), jnp.bfloat16),
            pltpu.VMEM((3 * 16, taps), jnp.bfloat16),
            pltpu.VMEM((3, 3, tiles // TURN, SUB, LANES), jnp.float32),
        ],
        name="deconvolve",
    )(ind_rows, col_frames, ind_taps, col_kernel, cell_u, cell_v, cell_w, tile_counts)
    arrived = lax.all_to_all(outgoing, "wire", split_axis=0, concat_axis=0, tiled=True)
    return pl.pallas_call(
        cell_kernel,
        out_shape=jax.ShapeDtypeStruct((1, 1, SUB, cell_u.shape[2]), jnp.float32),
        in_specs=[vmem] * 3,
        out_specs=vmem,
        name="cells",
        compiler_params=pltpu.CompilerParams(vmem_limit_bytes=4 << 20),
    )(arrived, wanted, extras)


def solution(mesh):
    return jax.shard_map(
        on_device,
        mesh=mesh,
        in_specs=(
            P("apa", None, "wire", None),
            P("apa", "wire", None),
            P(),
            P(),
            P("apa", "wire", None),
            P("apa", "wire", None),
            P("apa", "wire", None),
            P("apa", "wire"),
        ),
        out_specs=P("apa", "wire", None, None),
        check_vma=False,
    )
```

```python
import jax
import jax.numpy as jnp
from jax import lax
from jax.experimental import pallas as pl
from jax.experimental.pallas import tpu as pltpu
from jax.sharding import PartitionSpec as P

LANES = 128
SUB = 8
REBIN = 4
HALF = 16
GROUP = 32
TURN = LANES // GROUP
RIGHT = 0
LEFT = 16


def lane_iota():
    return lax.broadcasted_iota(jnp.int32, (SUB, LANES), 1)


def between(lanes, low, high):
    return (lanes >= low) & (lanes < high)


def conv_kernel(reach, widths, ind_hbm, col_hbm, indk_hbm, colk_hbm, u_hbm, v_hbm, w_hbm, count_hbm,
                out, where_out, extras, indf, colf, indk, colk, cells, count, sems, toep, wide, filters, moved, sums):
    copies = [pltpu.make_async_copy(source, target, sems.at[i]) for i, (source, target) in enumerate((
        (indk_hbm, indk), (colk_hbm, colk), (ind_hbm.at[0:256], indf.at[0:256]), (ind_hbm.at[256:400], indf.at[256:400]), (col_hbm.at[:, :, 0:512], colf.at[:, :, 0:512]), (col_hbm.at[:, :, 512:1024], colf.at[:, :, 512:1024]),
        (u_hbm, cells.at[0]), (v_hbm, cells.at[1]), (w_hbm, cells.at[2]), (count_hbm, count)))]
    for copy in copies:
        copy.start()
    offsets, taps = colk.shape
    ticks = colf.shape[2]
    window = taps + LANES
    blocks = ticks // LANES
    history = taps // LANES
    bins = LANES // REBIN
    pieces = window // LANES
    lanes = lane_iota()
    subs = lax.broadcasted_iota(jnp.int32, (SUB, LANES), 0)

    tap = lax.broadcasted_iota(jnp.int32, (taps, window), 0)
    column = lax.broadcasted_iota(jnp.int32, (taps, window), 1)
    total = tap + jnp.where(column < taps, column, taps + (column & (REBIN - 1)))
    fold = between(total, taps, taps + REBIN).astype(jnp.float32).astype(jnp.bfloat16)
    part_rows = 2 * blocks * HALF
    place = lax.broadcasted_iota(jnp.int32, (part_rows, part_rows), 0)
    source = lax.broadcasted_iota(jnp.int32, (part_rows, part_rows), 1)
    wanted = (place & (HALF - 1)) * (2 * blocks) + (place // HALF & (blocks - 1)) * 2 + place // (part_rows // 2)
    pick = (source == wanted).astype(jnp.float32).astype(jnp.bfloat16)

    stand = lax.axis_index("wire") // (bins // SUB) & (TURN - 1)
    group = (lanes // GROUP - stand) & (TURN - 1)
    slot = lanes & (GROUP - 1)
    for plane in range(3):
        width = widths[plane]
        first = slot < reach
        last = between(slot, width - reach, width)
        index = jnp.where(
            first, ((group - plane + 2 + stand) & (TURN - 1)) * GROUP + RIGHT + reach * plane + slot,
            ((group - plane + stand) & (TURN - 1)) * GROUP + LEFT + reach * plane + slot - (width - reach))
        extras[plane] = jnp.where(first | last, index, -1)

    filters[...] = jnp.zeros_like(filters)
    copies[0].wait()
    copies[1].wait()

    both = indk[...]
    for plane, k in enumerate((both[:, 0, :], both[:, 1, :], colk[...])):
        filters[16 * plane:16 * plane + offsets, :] = k
    all_rows = jnp.dot(filters[...], fold, preferred_element_type=jnp.float32)
    rows_of = [all_rows[16 * plane:16 * plane + offsets] for plane in range(3)]

    mine = lax.axis_index("wire") & (TURN - 1)
    group = (lanes // GROUP - mine) & (TURN - 1)
    in_group = [group == i for i in range(TURN)]
    slot = lanes & (GROUP - 1)
    per_half = LANES // GROUP

    def spread(plane, rows):
        width = widths[plane]
        blank = jnp.zeros((HALF, LANES), jnp.bfloat16)
        for part in range(GROUP // HALF):
            if plane < 2:
                at = plane * blocks
                tiles = [rows[part][HALF * (at + i):HALF * (at + i + 1)] for i in range(blocks)]
            else:
                count = min(HALF, width - HALF * part)
                mine = colf[0, HALF * part:HALF * part + count, :]
                if count < HALF:
                    mine = jnp.concatenate([mine, jnp.zeros((HALF - count, ticks), jnp.bfloat16)], axis=0)
                tiles = [mine[:, LANES * i:LANES * (i + 1)] for i in range(blocks)]
            for block, piece in enumerate([blank] * history + tiles):
                row = GROUP * block + HALF * part
                wide[plane, row:row + HALF, :] = piece

    def toeplitz(plane):
        for offset in range(offsets):
            row = rows_of[plane][offset:offset + 1, :]
            flat = [jnp.broadcast_to(row[:, LANES * i:LANES * (i + 1)], (SUB, LANES)) for i in range(pieces)]
            made = []
            for part in range(bins // SUB):
                base = part * SUB * REBIN
                shift = base + REBIN * subs
                turned = [pltpu.roll(piece, base, 1, stride=REBIN, stride_axis=0) for piece in flat[:-1]]
                own = jnp.where(lanes < shift + REBIN, flat[-1], 0.0)
                after = turned[1:] + [own]
                before = turned
                made.append([jnp.where(lanes >= shift, turned[0], 0.0)]
                            + [jnp.where(lanes >= shift, a, b) for a, b in zip(after, before)])
            for pair in range(0, len(made), 2):
                at_row = offset * bins + pair * SUB
                for i in range(pieces):
                    exact = jnp.concatenate([made[pair][i], made[pair + 1][i]], axis=0)
                    high = exact.astype(jnp.bfloat16)
                    low = (exact - high.astype(jnp.float32)).astype(jnp.bfloat16)
                    toep[plane, at_row:at_row + 16, LANES * i:LANES * (i + 1)] = high
                    toep[plane, at_row:at_row + 16, window + LANES * i:window + LANES * (i + 1)] = low

    def multiply(plane):
        seen = [wide[plane, GROUP * i:GROUP * (i + blocks), :] for i in range(pieces)]
        sums[plane] = lax.dot_general(
            toep[plane], jnp.concatenate(seen + seen, axis=1), (((1,), (1,)), ((), ())),
            preferred_element_type=jnp.float32)


    def shift_add(plane):
        for half in range(blocks // per_half):
            for part in range(bins // SUB):
                width = widths[plane]
                spare = GROUP - width

                def run(first, last):
                    acc = None
                    for shift in range(first, last + 1):
                        at_row = (reach - shift) * bins + part * SUB
                        piece = sums[plane, at_row:at_row + SUB, LANES * half:LANES * (half + 1)]
                        piece = piece if shift == 0 else pltpu.roll(piece, shift % LANES, 1)
                        acc = piece if acc is None else acc + piece
                    return acc

                if spare >= reach:
                    after, before = run(0, reach), run(-reach, -1)
                    main = after + before
                else:
                    near, far = run(0, spare), run(spare + 1, reach)
                    main = near + jnp.where(slot > spare, far, 0.0)
                    after = jnp.where(slot >= width, near, 0.0) + far
                    near, far = run(-spare, -1), run(-reach, -spare - 1)
                    main = main + near + jnp.where(slot < GROUP - reach, far, 0.0)
                    before = jnp.where(slot >= width, near, 0.0) + far
                main = pltpu.roll(main, ((plane + mine) & (TURN - 1)) * GROUP, 1)
                for i, value in enumerate((main, after, before)):
                    moved[plane, i, half * (bins // SUB) + part] = value

    for copy in copies[2:]:
        copy.wait()
    rows = [jnp.dot(pick[:, :min(part_rows, indf.shape[0] - at)], indf[at:min(at + part_rows, indf.shape[0]), :],
                    preferred_element_type=jnp.float32).astype(jnp.bfloat16)
            for at in range(0, indf.shape[0], part_rows)]
    for plane in range(3):
        spread(plane, rows)
        toeplitz(plane)
    for plane in range(3):
        multiply(plane)
    for plane in range(3):
        shift_add(plane)

    stand = lax.axis_index("wire") // (bins // SUB) & (TURN - 1)
    for plane in range(3):
        width = widths[plane]
        for chunk in range(cells.shape[3] // LANES):
            span = slice(chunk * LANES, (chunk + 1) * LANES)
            wire = jnp.broadcast_to(cells[plane, 0, 0:1, span], (SUB, LANES))
            owner = (wire * ((1 << 18) // width + 1)) >> 18
            spot = wire - owner * width + ((owner + plane + stand) & (TURN - 1)) * GROUP
            spot = spot + (owner // TURN) * LANES
            live = lanes + chunk * LANES < count[0, 0]
            where_out[plane, :, span] = jnp.where(live, spot, -1)


    edge = ((TURN - 1 + mine) & (TURN - 1)) * GROUP
    for half in range(blocks // per_half):
        for part in range(bins // SUB):
            step = half * (bins // SUB) + part
            turned = [moved[plane, 0, step] for plane in range(3)]
            edges, halo = [], None
            for plane in range(3):
                edges += [(RIGHT + reach * plane, widths[plane], moved[plane, 1, step]),
                          (LEFT + reach * plane, -reach, moved[plane, 2, step])]
            for target, begin, acc in sorted(edges, key=lambda item: item[0]):
                placed = pltpu.roll(acc, (edge + (target - begin) % LANES) & (LANES - 1), 1)
                halo = placed if halo is None else jnp.where(slot >= target, placed, halo)
            turned.append(halo)
            for spot in range(per_half):
                tile = (half * per_half + spot) * (bins // SUB) + part
                result = turned[0]
                for plane in range(1, TURN):
                    result = jnp.where(in_group[(spot + plane) % TURN], turned[plane], result)
                out[tile] = result


def cell_kernel(table, wanted, extras, out):
    sources = table.shape[0]
    lanes = lane_iota()
    stand = lax.axis_index("wire") // (LANES // REBIN // SUB) & (TURN - 1)
    group = (lanes // GROUP - stand) & (TURN - 1)
    slot = lanes & (GROUP - 1)
    zero = jnp.zeros((SUB, LANES), jnp.float32)

    def joined(stage, plane):
        made = None
        for i in range(TURN):
            piece = table[stage * TURN + i]
            made = piece if made is None else jnp.where(group == (plane + i) % TURN, piece, made)
        return made

    stages = sources // TURN
    halos = [joined(stage, TURN - 1) for stage in range(stages)]
    early = (group == TURN - 2) & (slot < LEFT)
    late = (group == TURN - 1) & (slot >= LEFT)
    mixed = []
    for stage in range(stages):
        made = jnp.where(early, halos[stage - 1] if stage > 0 else zero, halos[stage])
        mixed.append(jnp.where(late, halos[stage + 1] if stage + 1 < stages else zero, made))
    full = []
    for plane in range(3):
        index = extras[plane]
        added = index >= 0
        index = index & (LANES - 1)
        full.append([joined(stage, plane) + jnp.where(
            added, jnp.take_along_axis(mixed[stage], index, axis=1), 0.0) for stage in range(stages)])

    for chunk in range(wanted.shape[2] // LANES):
        span = slice(chunk * LANES, (chunk + 1) * LANES)
        charge = None
        for plane in range(3):
            at = wanted[plane, :, span]
            stage_of, lane_of = at >> 7, at & (LANES - 1)
            picked = zero
            for stage in range(stages):
                value = jnp.take_along_axis(full[plane][stage], lane_of, axis=1)
                picked = jnp.where(stage_of == stage, value, picked)
            charge = picked if charge is None else jnp.minimum(charge, picked)
        out[0, 0, :, span] = charge


def on_device(ind_frames, col_frames, ind_kernel, col_kernel, cell_u, cell_v, cell_w, tile_counts):
    offsets, taps = col_kernel.shape
    reach = (offsets - 1) // 2
    ticks = ind_frames.shape[3]
    widths = (ind_frames.shape[2], ind_frames.shape[2], col_frames.shape[1])
    bins = LANES // REBIN
    tiles = ticks // REBIN // SUB
    window = taps + LANES
    blocks = ticks // LANES
    ind_rows = ind_frames.reshape(2, widths[0], blocks, LANES).transpose(1, 2, 0, 3).reshape(-1, LANES)
    ind_taps = ind_kernel.transpose(1, 0, 2)
    vmem = pl.BlockSpec(memory_space=pltpu.VMEM)
    outgoing, wanted, extras = pl.pallas_call(
        lambda *refs: conv_kernel(reach, widths, *refs),
        out_shape=(pltpu.VMEM((tiles, SUB, LANES), jnp.float32),
                   pltpu.VMEM((3, SUB, cell_u.shape[2]), jnp.int32),
                   pltpu.VMEM((3, SUB, LANES), jnp.int32)),
        in_specs=[pl.BlockSpec(memory_space=pltpu.HBM)] * 8,
        out_specs=(vmem, vmem, vmem),
        scratch_shapes=[
            pltpu.VMEM(ind_rows.shape, jnp.bfloat16),
            pltpu.VMEM(col_frames.shape, jnp.bfloat16),
            pltpu.VMEM(ind_taps.shape, jnp.bfloat16),
            pltpu.VMEM(col_kernel.shape, jnp.bfloat16),
            pltpu.VMEM((3,) + cell_u.shape[0:], jnp.int32),
            pltpu.SMEM(tile_counts.shape, jnp.int32),
            pltpu.SemaphoreType.DMA((10,)),
            pltpu.VMEM((3, offsets * bins, 2 * window), jnp.bfloat16),
            pltpu.VMEM((3, GROUP * (blocks + taps // LANES), LANES), jnp.bfloat16),
            pltpu.VMEM((3 * 16, taps), jnp.bfloat16),
            pltpu.VMEM((3, 3, tiles // TURN, SUB, LANES), jnp.float32),
            pltpu.VMEM((3, offsets * bins, GROUP * blocks), jnp.float32),
        ],
        name="deconvolve",
    )(ind_rows, col_frames, ind_taps, col_kernel, cell_u, cell_v, cell_w, tile_counts)
    arrived = lax.all_to_all(outgoing, "wire", split_axis=0, concat_axis=0, tiled=True)
    return pl.pallas_call(
        cell_kernel,
        out_shape=jax.ShapeDtypeStruct((1, 1, SUB, cell_u.shape[2]), jnp.float32),
        in_specs=[vmem] * 3,
        out_specs=vmem,
        name="cells",
        compiler_params=pltpu.CompilerParams(vmem_limit_bytes=4 << 20),
    )(arrived, wanted, extras)


def solution(mesh):
    return jax.shard_map(
        on_device,
        mesh=mesh,
        in_specs=(
            P("apa", None, "wire", None),
            P("apa", "wire", None),
            P(),
            P(),
            P("apa", "wire", None),
            P("apa", "wire", None),
            P("apa", "wire", None),
            P("apa", "wire"),
        ),
        out_specs=P("apa", "wire", None, None),
        check_vma=False,
    )
```
